32 devices in a mesh: dp: 8 (over y, x, core), seq: 4 (over z).
Axes of the slice: x: 2, y: 2, z: 4, core: 2. Of those that a mesh axis runs over, the one named last changes fastest.
Arguments:
- queries: bfloat16 [8, 4, 384, 1024], P('dp', 'seq'), may hold values from -6 to 6
- keys: bfloat16 [8, 4, 384, 1024], P('dp', 'seq'), may hold values from -6 to 6
- values: bfloat16 [8, 4, 384, 1024], P('dp', 'seq'), may hold values from -6 to 6
- gates: bfloat16 [8, 4, 384, 1024], P('dp', 'seq'), may hold values from -6 to 6
- attended: bfloat16 [8, 4, 384, 1024], P('dp', 'seq')
- out_grad: bfloat16 [8, 4, 384, 1024], P('dp', 'seq'), may hold values from -6 to 6
- plan: int32 [8, 4, 8], P(None, 'seq'), may hold values from 1 to 48, 256 in all within a row
- hist_len: int32 [8], P('dp'), may hold values from 256 to 1024, as said below
- block_mask: int32 [8, 8, 8], P('dp'), may hold values 0 or 1
Outputs:
- query_grad: bfloat16 [8, 4, 384, 1024], P('dp', 'seq')
- key_grad: bfloat16 [8, 4, 384, 1024], P('dp', 'seq')
- value_grad: bfloat16 [8, 4, 384, 1024], P('dp', 'seq')
- gate_grad: bfloat16 [8, 4, 384, 1024], P('dp', 'seq')
The draws below stay inside these ranges and needn't reach their ends.
Inputs may be any that keep to these rules, and one draw needn't show every extreme that they name: For every history g and piece s, plan[g, s, :] sums to 256; some entry of each such row equals 48. `hist_len`: some history has exactly 1024 events.
All inputs are finite; a program needn't handle non-finite values. No bound on the sum of `block_mask` on one device may be relied on, other than what follows from the above.
Results may differ from the reference program's by a relative error of at most 0.0058.
Values may be sent and summed in bfloat16 or wider, within the bound.
No kernel may reach another device: no remote copies, remote signals or barrier semaphores. Data moves between devices by JAX's collectives and lax.ppermute only.
A program may use at most 128 MiB of HBM per device.

```python
import math
import jax
import jax.numpy as jnp
import numpy as np
from jax import lax

D = 1024
HEADS = 8
DH = 128
ROWS = 256
BLOCK = 128
GROUPS = 8
PIECES = 4
SLOT = 48
CAP = 384
LEN = 1024
NBLK = 8


def draw_hist_len(key, part):
    first_key, second_key = jax.random.split(key)
    lengths = jax.random.randint(first_key, (GROUPS,), LEN // 4, LEN + 1)
    chosen = jax.random.randint(second_key, (), 0, GROUPS)
    return jnp.where(jnp.arange(GROUPS) == chosen, LEN, lengths).astype(jnp.int32)


def draw_attended(key, part):
    key_list = jax.random.split(key, 3)
    row_scale = jnp.exp(jax.random.uniform(key_list[1], (GROUPS, PIECES, CAP, 1), jnp.float32, 0.0, math.log(10.0)))
    col_scale = jnp.exp(jax.random.uniform(key_list[2], (D,), jnp.float32, 0.0, math.log(10.0)))
    base = jax.random.normal(key_list[0], (GROUPS, PIECES, CAP, D), jnp.float32)
    result = row_scale * col_scale * base
    return result.astype(jnp.bfloat16)


def plant(values, own_key, low, top_value):
    extent = values.shape
    index_at = [jax.random.randint(jax.random.fold_in(own_key, axis), (), 0, extent[axis]) for axis in range(len(extent))]
    values = values.at[tuple(index_at)].set(low)
    longest = extent.index(max(extent))
    index_at[longest] = (index_at[longest] + 1) % extent[longest]
    return values.at[tuple(index_at)].set(top_value)


def steps_of(rng, shape, shards, smallest, top_value):
    level = 1.0
    for axis_at, blocks in shards:
        draws = jax.random.uniform(jax.random.fold_in(jax.random.fold_in(rng, 6), axis_at), (blocks,), jnp.float32, smallest / len(shards), top_value / len(shards))
        level = level * jnp.repeat(jnp.exp(draws), shape[axis_at] // blocks).reshape((-1,) + (1,) * (len(shape) - 1 - axis_at))
    return level


def profile(count, total, reach, lean):
    loads = [(1 << 20) // math.isqrt(grade ** lean) + 1 for grade in range(2, count + 1)]
    surplus, holding = total - reach - (count - 1), [1] * (count - 1)
    while surplus > 0:
        candidates = [i for i in range(count - 1) if holding[i] < reach]
        whole, left = sum([loads[i] for i in candidates]), surplus
        for i in candidates:
            addition = min(reach - holding[i], max(1, left * loads[i] // whole), surplus)
            holding[i] = holding[i] + addition
            surplus = surplus - addition
    return np.array([reach] + holding)


def ragged_sizes(key, count, total, bound, slope):
    if count == 2:
        one = jax.random.randint(key, (), max(1, total - bound), min(bound, total - 1) + 1)
        return jnp.stack([one, total - one])
    sizes = jnp.asarray(profile(count, total, bound, slope), jnp.int32)
    twos = (count - 1) // 2
    giver, sink = sizes[1:1 + 2 * twos:2], sizes[2:2 + 2 * twos:2]
    slack = jnp.minimum(giver - 1, bound - sink)
    shifted = jax.random.randint(jax.random.fold_in(key, 1), (twos,), 0, 1 << 20) % (slack + 1)
    sizes = sizes.at[1:1 + 2 * twos:2].set(giver - shifted).at[2:2 + 2 * twos:2].set(sink + shifted)
    return sizes[jax.random.permutation(jax.random.fold_in(key, 2), count)]


def gaussian(own_key, extent, deviation, limit, cuts=(), kind=jnp.bfloat16):
    values = jax.random.normal(own_key, extent, jnp.float32) * deviation
    if len(cuts) > 0:
        values = steps_of(own_key, extent, cuts, -0.22, 0.18) * values
    return jnp.clip(values, min=-limit, max=limit).astype(kind)


def setup_inputs(seed: int = 0) -> dict:
    splits = jax.random.split(jax.random.key(seed), 10)
    queries = gaussian(splits[0], (GROUPS, PIECES, CAP, D), 1.0, 6.0, ((0, 8), (1, 4)))
    keys = gaussian(splits[1], (GROUPS, PIECES, CAP, D), 1.0, 6.0, ((0, 8), (1, 4)))
    values = gaussian(splits[2], (GROUPS, PIECES, CAP, D), 1.0, 6.0, ((0, 8), (1, 4)))
    gates = gaussian(splits[3], (GROUPS, PIECES, CAP, D), 1.0, 6.0, ((0, 8), (1, 4)))
    attended = draw_attended(jax.random.fold_in(splits[9], 71), 0)
    out_grad = gaussian(splits[5], (GROUPS, PIECES, CAP, D), 1.0, 6.0, ((0, 8), (1, 4)))
    plan = jax.vmap(lambda own: ragged_sizes(own, GROUPS, ROWS, SLOT, 2))(jax.random.split(splits[6], GROUPS * PIECES)).reshape((GROUPS, PIECES, GROUPS)).astype(jnp.int32)
    hist_len = draw_hist_len(jax.random.fold_in(splits[9], 71), 0)
    block_mask = plant((jax.random.randint(splits[8], (GROUPS, NBLK, NBLK), 0, 2) < 1).astype(jnp.int32), jax.random.fold_in(splits[8], 1), 0, 1)
    return {"queries": queries, "keys": keys, "values": values, "gates": gates, "attended": attended, "out_grad": out_grad, "plan": plan, "hist_len": hist_len, "block_mask": block_mask}


def layer_norm(inputs):
    center = inputs - lax.optimization_barrier(jnp.mean(inputs, axis=-1, keepdims=True))
    spread = lax.optimization_barrier(jnp.mean(center * center, axis=-1, keepdims=True))
    return center * lax.rsqrt(spread + 1e-05)

def head_terms(query_rows, key_rows, value_rows, grad_rows, live_weight):
    scale_qk = DH ** (-0.5)
    scores = jnp.dot(query_rows, key_rows.T, preferred_element_type=jnp.float32) * scale_qk
    sigmoid = jax.nn.sigmoid(scores)
    weight = (scores * sigmoid * live_weight).astype(jnp.bfloat16)
    products = jnp.dot(grad_rows, value_rows.T, preferred_element_type=jnp.float32)
    score_grad = (products * (sigmoid * (1.0 + scores * (1.0 - sigmoid))) * live_weight).astype(jnp.bfloat16)
    query_part = jnp.dot(score_grad, key_rows, preferred_element_type=jnp.float32) * scale_qk
    key_part = jnp.dot(score_grad.T, query_rows, preferred_element_type=jnp.float32) * scale_qk
    value_part = jnp.dot(weight.T, grad_rows, preferred_element_type=jnp.float32)
    return (query_part, key_part, value_part)

def group_terms(operands):
    query_all, key_all, value_all, grad_all, length, pattern = operands
    positions = jnp.arange(LEN, dtype=jnp.int32)
    block_of = positions // BLOCK
    onehot = (block_of[:, None] == jnp.arange(NBLK, dtype=jnp.int32)[None, :]).astype(jnp.float32)
    blocks = jnp.dot(jnp.dot(onehot, pattern.astype(jnp.float32), precision=lax.Precision.HIGHEST), onehot.T, precision=lax.Precision.HIGHEST)
    keep = (positions[None, :] <= positions[:, None]) & (positions[:, None] < length) & (positions[None, :] < length)
    keep = keep & ((blocks > 0.5) | (block_of[:, None] == block_of[None, :]))
    inverse = 1.0 / jnp.sqrt(length.astype(jnp.float32))
    live_weight = keep.astype(jnp.float32) * inverse

    def one_head(parts):
        return head_terms(parts[0], parts[1], parts[2], parts[3], live_weight)
    return lax.map(one_head, (query_all, key_all, value_all, grad_all))

def reference(queries, keys, values, gates, attended, out_grad, plan, hist_len, block_mask):
    normed, pullback = jax.vjp(layer_norm, attended.astype(jnp.float32))
    cotangent = out_grad.astype(jnp.float32) * gates.astype(jnp.float32)
    attn_grad = pullback(cotangent)[0].astype(jnp.bfloat16)
    plan = plan.astype(jnp.int32)
    cum_incl = jnp.cumsum(plan, axis=2).astype(jnp.int32)
    cum_excl = (cum_incl - plan).astype(jnp.int32)
    slot_ids = jnp.arange(SLOT, dtype=jnp.int32)
    incoming = jnp.transpose(plan, (2, 1, 0))
    valid = (slot_ids[None, None, None, :] < incoming[..., None]).reshape(GROUPS, PIECES, CAP)
    gate_grad = jnp.where(valid[..., None], out_grad.astype(jnp.float32) * normed, 0.0).astype(jnp.bfloat16)
    row_ids = jnp.arange(ROWS, dtype=jnp.int32)
    dest = lax.optimization_barrier(jnp.sum((cum_incl[:, :, None, :] <= row_ids[None, None, :, None]).astype(jnp.int32), axis=3)).astype(jnp.int32)
    begin = jnp.take_along_axis(cum_excl, dest, axis=2).astype(jnp.int32)
    group_ids = jnp.arange(GROUPS, dtype=jnp.int32)
    slot_index = (group_ids[:, None, None] * SLOT + row_ids[None, None, :] - begin).astype(jnp.int32)
    piece_index = jnp.arange(PIECES, dtype=jnp.int32)[None, :, None]

    def to_history(array):
        picked = array[dest, piece_index, slot_index]
        return picked.reshape(GROUPS, LEN, HEADS, DH).transpose(0, 2, 1, 3)
    histories = (to_history(queries), to_history(keys), to_history(values), to_history(attn_grad))
    grads = lax.map(group_terms, (histories[0], histories[1], histories[2], histories[3], hist_len.astype(jnp.int32), block_mask.astype(jnp.int32)))
    row_index = jnp.minimum(jnp.transpose(cum_excl, (2, 1, 0))[..., None] + slot_ids, ROWS - 1).astype(jnp.int32)
    group_index = group_ids[None, None, :, None]
    piece_back = jnp.arange(PIECES, dtype=jnp.int32)[None, :, None, None]

    def to_slots(history):
        rows_view = history.transpose(0, 2, 1, 3).reshape(GROUPS, PIECES, ROWS, D)
        picked = rows_view[group_index, piece_back, row_index].reshape(GROUPS, PIECES, CAP, D)
        return jnp.where(valid[..., None], picked, 0.0).astype(jnp.bfloat16)
    return (to_slots(grads[0]), to_slots(grads[1]), to_slots(grads[2]), gate_grad)
```

```python
import functools

import jax
import jax.numpy as jnp
from jax import lax
from jax.experimental import pallas as pl
from jax.experimental.pallas import tpu as pltpu
from jax.sharding import PartitionSpec as P

HEADS = 8
ROWS = 256
BLOCK = 128


VMEM_SPEC = pl.BlockSpec(memory_space=pltpu.VMEM)
SMEM_SPEC = pl.BlockSpec(memory_space=pltpu.SMEM)
NT = (((1,), (1,)), ((), ()))
TN = (((0,), (0,)), ((), ()))


def layer_norm(inputs):
    center = inputs - jnp.mean(inputs, axis=-1, keepdims=True)
    spread = jnp.mean(center * center, axis=-1, keepdims=True)
    return center * lax.rsqrt(spread + 1e-05)


def flatten(array):
    return array.reshape(array.shape[2], array.shape[3])


def unpack_kernel(place_ref, select_ref, rows_ref, *out_refs):
    me = place_ref[0]
    width = out_refs[0].shape[1]
    for step, out_ref in enumerate(out_refs):
        start = pl.multiple_of((me ^ step) * width, width)
        out_ref[...] = jnp.dot(
            select_ref[...], rows_ref[:, pl.ds(start, width)], preferred_element_type=jnp.float32
        ).astype(out_ref.dtype)


def pack_kernel(place_ref, select_ref, *refs):
    me = place_ref[0]
    out_ref = refs[-1]
    width = refs[0].shape[1]
    for step, block_ref in enumerate(refs[:-1]):
        start = pl.multiple_of((me ^ step) * width, width)
        out_ref[:, pl.ds(start, width)] = jnp.dot(
            select_ref[...], block_ref[...], preferred_element_type=jnp.float32
        ).astype(out_ref.dtype)


def gather_blocks(me, block_refs, scratch_ref):
    rows = block_refs[0].shape[0]
    for step, block_ref in enumerate(block_refs):
        scratch_ref[pl.ds(pl.multiple_of((me ^ step) * rows, rows), rows), :] = block_ref[...]


def spread_blocks(me, scratch_ref, out_refs):
    rows = out_refs[0].shape[0]
    for step, out_ref in enumerate(out_refs):
        start = pl.multiple_of((me ^ step) * rows, rows)
        out_ref[...] = scratch_ref[pl.ds(start, rows), :].astype(out_ref.dtype)


def live_tile(place_ref, mask_ref, inverse, query_start, key_start, rows):
    length = place_ref[1]
    row_ids = lax.broadcasted_iota(jnp.int32, (rows, rows), 0)
    column_ids = lax.broadcasted_iota(jnp.int32, (rows, rows), 1)
    key_pos = key_start + row_ids
    query_pos = query_start + column_ids
    blocks = rows // BLOCK
    allowed = jnp.zeros((rows, rows), jnp.int32)
    for key_sub in range(blocks):
        for query_sub in range(blocks):
            key_block = key_start // BLOCK + key_sub
            query_block = query_start // BLOCK + query_sub
            flag = jnp.where(key_block == query_block, 1, mask_ref[query_block, key_block])
            here = (row_ids // BLOCK == key_sub) & (column_ids // BLOCK == query_sub)
            allowed = jnp.where(here, flag, allowed)
    keep = (key_pos <= query_pos) & (query_pos < length) & (allowed > 0)
    return jnp.where(keep, inverse, 0.0)


def silu_terms(query_tile, key_tile):
    scores = lax.dot_general(
        key_tile, query_tile, NT, preferred_element_type=jnp.float32
    ) * (query_tile.shape[1] ** (-0.5))
    return scores, 1.0 / (1.0 + jnp.exp(-scores))


def tile_loop(pieces, body):
    def outer(query_piece, carry):
        def inner(key_piece, carry):
            body(query_piece, key_piece)
            return carry

        return lax.fori_loop(0, query_piece + 1, inner, carry)

    lax.fori_loop(0, pieces, outer, 0)


def weight_kernel(pieces, heads, place_ref, inverse_ref, mask_ref, *refs):
    query_refs, key_refs = refs[:pieces], refs[pieces : 2 * pieces]
    weight_ref, query_all, key_all = refs[2 * pieces :]
    me = place_ref[0]
    rows = query_refs[0].shape[0]
    size = query_all.shape[1] // heads
    gather_blocks(me, query_refs, query_all)
    gather_blocks(me, key_refs, key_all)
    inverse = inverse_ref[0]

    def body(query_piece, key_piece):
        query_start = pl.multiple_of(query_piece * rows, rows)
        key_start = pl.multiple_of(key_piece * rows, rows)
        live = live_tile(place_ref, mask_ref, inverse, query_start, key_start, rows)
        for head in range(heads):
            columns = pl.ds(head * size, size)
            scores, sigmoid = silu_terms(
                query_all[pl.ds(query_start, rows), columns],
                key_all[pl.ds(key_start, rows), columns],
            )
            weight_ref[head, pl.ds(key_start, rows), pl.ds(query_start, rows)] = (
                scores * sigmoid * live
            ).astype(weight_ref.dtype)

    tile_loop(pieces, body)


def value_kernel(pieces, heads, place_ref, weight_ref, *refs):
    grad_refs = refs[:pieces]
    out_refs = refs[pieces : 2 * pieces]
    grad_all, value_all = refs[2 * pieces :]
    me = place_ref[0]
    rows = grad_refs[0].shape[0]
    size = grad_all.shape[1] // heads
    gather_blocks(me, grad_refs, grad_all)
    for head in range(heads):
        columns = slice(head * size, (head + 1) * size)
        for piece in range(pieces):
            value_all[piece * rows : (piece + 1) * rows, columns] = jnp.dot(
                weight_ref[head, piece * rows : (piece + 1) * rows, piece * rows :],
                grad_all[piece * rows :, columns],
                preferred_element_type=jnp.float32,
            )
    spread_blocks(me, value_all, out_refs)


def score_kernel(pieces, heads, place_ref, inverse_ref, mask_ref, *refs):
    groups = [refs[index * pieces : (index + 1) * pieces] for index in range(6)]
    query_all, key_all, value_all, grad_all, query_sum, key_sum = refs[6 * pieces :]
    me = place_ref[0]
    rows = groups[0][0].shape[0]
    size = query_all.shape[1] // heads
    scale = size ** (-0.5)
    for blocks, scratch in zip(groups[:4], (query_all, key_all, value_all, grad_all)):
        gather_blocks(me, blocks, scratch)
    query_sum[...] = jnp.zeros_like(query_sum)
    key_sum[...] = jnp.zeros_like(key_sum)
    inverse = inverse_ref[0]

    def body(query_piece, key_piece):
        query_start = pl.multiple_of(query_piece * rows, rows)
        key_start = pl.multiple_of(key_piece * rows, rows)
        query_rows = pl.ds(query_start, rows)
        key_rows = pl.ds(key_start, rows)
        live = live_tile(place_ref, mask_ref, inverse, query_start, key_start, rows)
        for head in range(heads):
            columns = pl.ds(head * size, size)
            query_tile = query_all[query_rows, columns]
            key_tile = key_all[key_rows, columns]
            scores, sigmoid = silu_terms(query_tile, key_tile)
            products = lax.dot_general(
                value_all[key_rows, columns],
                grad_all[query_rows, columns],
                NT,
                preferred_element_type=jnp.float32,
            )
            score_grad = (
                products * (sigmoid * (1.0 + scores * (1.0 - sigmoid))) * live
            ).astype(jnp.bfloat16)
            key_sum[key_rows, columns] += (
                jnp.dot(score_grad, query_tile, preferred_element_type=jnp.float32) * scale
            )
            query_sum[query_rows, columns] += (
                lax.dot_general(score_grad, key_tile, TN, preferred_element_type=jnp.float32)
                * scale
            )

    tile_loop(pieces, body)
    spread_blocks(me, query_sum, groups[4])
    spread_blocks(me, key_sum, groups[5])


def local(queries, keys, values, gates, attended, out_grad, plan, hist_len, block_mask):
    group_count = lax.axis_size("dp")
    piece_count = lax.axis_size("seq")
    capacity = queries.shape[2]
    model_width = queries.shape[3]
    slot_count = capacity // group_count
    row_count = ROWS
    head_per = HEADS // piece_count
    head_size = model_width // HEADS
    width = head_per * head_size
    full_len = row_count * piece_count
    dp_index = lax.axis_index("dp")
    shape_slots = (group_count, slot_count, model_width)
    group_ids = jnp.arange(group_count, dtype=jnp.int32)
    slot_ids = jnp.arange(slot_count, dtype=jnp.int32)
    my_plan = plan[:, 0, :]
    incoming = jnp.sum(jnp.where(group_ids[None, :] == dp_index, my_plan, 0), axis=1)
    valid = (slot_ids[None, :] < incoming[:, None]).reshape(capacity)
    own_counts = jnp.sum(jnp.where(group_ids[:, None] == dp_index, my_plan, 0), axis=0)
    before = jnp.sum(
        jnp.where(group_ids[:, None] < group_ids[None, :], own_counts[:, None], 0), axis=0
    )
    slot_rows = jnp.where(
        slot_ids[None, :] < own_counts[:, None], before[:, None] + slot_ids[None, :], -1
    ).reshape(capacity)
    row_ids = jnp.arange(row_count, dtype=jnp.int32)
    to_rows = (slot_rows[None, :] == row_ids[:, None]).astype(jnp.bfloat16)
    to_slots = (slot_rows[:, None] == row_ids[None, :]).astype(jnp.bfloat16)
    length = hist_len[0]
    place = jnp.stack([lax.axis_index("seq").astype(jnp.int32), length])
    inverse = (1.0 / jnp.sqrt(length.astype(jnp.float32))).reshape(1)
    mask = block_mask[0]

    def over_dp(array):
        return lax.all_to_all(
            array.reshape(shape_slots), "dp", split_axis=0, concat_axis=0, tiled=True
        ).reshape(capacity, model_width)

    def over_seq(blocks):
        result = [blocks[0]]
        for step in range(1, piece_count):
            pairs = [(source, source ^ step) for source in range(piece_count)]
            result.append(lax.ppermute(blocks[step], "seq", pairs))
        return result

    block_shape = jax.ShapeDtypeStruct((row_count, width), jnp.bfloat16)
    all_bf16 = pltpu.VMEM((full_len, width), jnp.bfloat16)
    all_f32 = pltpu.VMEM((full_len, width), jnp.float32)

    def unpack(array):
        return pl.pallas_call(
            unpack_kernel,
            out_shape=[block_shape] * piece_count,
            in_specs=[SMEM_SPEC, VMEM_SPEC, VMEM_SPEC],
            out_specs=[VMEM_SPEC] * piece_count,
            name="unpack",
        )(place, to_rows, array)

    def pack(blocks):
        return pl.pallas_call(
            pack_kernel,
            out_shape=jax.ShapeDtypeStruct((capacity, model_width), jnp.bfloat16),
            in_specs=[SMEM_SPEC] + [VMEM_SPEC] * (1 + piece_count),
            out_specs=VMEM_SPEC,
            name="pack",
        )(place, to_slots, *blocks)

    normed, pullback = jax.vjp(layer_norm, flatten(attended).astype(jnp.float32))
    cotangent = flatten(out_grad).astype(jnp.float32) * flatten(gates).astype(jnp.float32)
    attn_grad = pullback(cotangent)[0].astype(jnp.bfloat16)
    gate_grad = jnp.where(
        valid[:, None], flatten(out_grad).astype(jnp.float32) * normed, 0.0
    ).astype(jnp.bfloat16)

    histories = [
        over_seq(unpack(over_dp(array)))
        for array in (flatten(queries), flatten(keys), flatten(values), attn_grad)
    ]
    query_blocks, key_blocks, value_blocks, grad_blocks = histories

    weight = pl.pallas_call(
        functools.partial(weight_kernel, piece_count, head_per),
        out_shape=jax.ShapeDtypeStruct((head_per, full_len, full_len), jnp.bfloat16),
        in_specs=[SMEM_SPEC] * 3 + [VMEM_SPEC] * (2 * piece_count),
        out_specs=VMEM_SPEC,
        scratch_shapes=[all_bf16] * 2,
        name="weight",
    )(place, inverse, mask, *query_blocks, *key_blocks)
    value_grads = pl.pallas_call(
        functools.partial(value_kernel, piece_count, head_per),
        out_shape=[block_shape] * piece_count,
        in_specs=[SMEM_SPEC] + [VMEM_SPEC] * (1 + piece_count),
        out_specs=[VMEM_SPEC] * piece_count,
        scratch_shapes=[all_bf16, all_f32],
        name="value",
    )(place, weight, *grad_blocks)
    score_grads = pl.pallas_call(
        functools.partial(score_kernel, piece_count, head_per),
        out_shape=[block_shape] * (2 * piece_count),
        in_specs=[SMEM_SPEC] * 3 + [VMEM_SPEC] * (4 * piece_count),
        out_specs=[VMEM_SPEC] * (2 * piece_count),
        scratch_shapes=[all_bf16] * 4 + [all_f32] * 2,
        name="score",
    )(place, inverse, mask, *query_blocks, *key_blocks, *value_blocks, *grad_blocks)

    out_shape = (1, 1, capacity, model_width)
    value_out = over_dp(pack(over_seq(value_grads)))
    query_out = over_dp(pack(over_seq(score_grads[:piece_count])))
    key_out = over_dp(pack(over_seq(score_grads[piece_count:])))
    return (
        query_out.reshape(out_shape),
        key_out.reshape(out_shape),
        value_out.reshape(out_shape),
        gate_grad.reshape(out_shape),
    )


def solution(mesh):
    rows_spec = P("dp", "seq", None, None)
    in_specs = (rows_spec,) * 6 + (P(None, "seq", None), P("dp"), P("dp", None, None))
    return jax.shard_map(
        local, mesh=mesh, in_specs=in_specs, out_specs=(rows_spec,) * 4, check_vma=False
    )
```

```python
import functools

import jax
import jax.numpy as jnp
from jax import lax
from jax.experimental import pallas as pl
from jax.experimental.pallas import tpu as pltpu
from jax.sharding import PartitionSpec as P


HEADS = 8
ROWS = 256
BLOCK = 128
TILE = 16


WHOLE = ("q", "g", "dv")

VMEM_SPEC = pl.BlockSpec(memory_space=pltpu.VMEM)
SMEM_SPEC = pl.BlockSpec(memory_space=pltpu.SMEM)
ANY_SPEC = pl.BlockSpec(memory_space=pl.ANY)
NT = (((1,), (1,)), ((), ()))
TN = (((0,), (0,)), ((), ()))


def size_of(array):
    return array.size * array.dtype.itemsize


def call(kernel, inputs, outputs, scratch=(), scalars=0, any_space=False):
    space = ANY_SPEC if any_space else VMEM_SPEC
    held = sum(size_of(array) for array in list(inputs[scalars:]) + list(outputs))
    held += sum(
        ref.inner_aval.size * ref.inner_aval.dtype.itemsize for ref in scratch if not any_space
    )
    results = pl.pallas_call(
        kernel,
        out_shape=outputs,
        in_specs=[SMEM_SPEC] * scalars + [space] * (len(inputs) - scalars),
        out_specs=[space] * len(outputs),
        scratch_shapes=list(scratch),
        compiler_params=pltpu.CompilerParams(vmem_limit_bytes=held + (6 << 20)),
    )(*inputs)
    return list(results)


def aligned(index, size):
    return pl.ds(pl.multiple_of(index * size, size), size)


def select_matrix(count_at, mixed, group_count, slot_pad, rows):
    capacity = group_count * slot_pad
    lanes = lax.broadcasted_iota(jnp.int32, (1, capacity), 1)
    before = []
    total = jnp.int32(0)
    for group in range(group_count):
        before.append(total)
        total = total + count_at(jnp.int32(group))
    slot_rows = jnp.full((1, capacity), -1, jnp.int32)
    for place in range(group_count):
        group = mixed ^ place
        start = jnp.int32(0)
        for other in range(group_count):
            start = jnp.where(group == other, before[other], start)
        slot = lanes - place * slot_pad
        inside = (slot >= 0) & (slot < count_at(group))
        slot_rows = jnp.where(inside, start + slot, slot_rows)
    row_ids = lax.broadcasted_iota(jnp.int32, (rows, capacity), 0)
    return (row_ids == slot_rows).astype(jnp.float32).astype(jnp.bfloat16)


def split_kernel(place_ref, rows_ref, plan_ref, *out_refs):
    me = place_ref[0]
    capacity = rows_ref.shape[0]
    width = out_refs[0].shape[1]
    for step, out_ref in enumerate(out_refs):
        out_ref[:capacity, :] = rows_ref[:, aligned(me ^ step, width)]
        out_ref[capacity:, :] = plan_ref[...]


def norm_kernel(
    group_count, permuted, place_ref, plan_ref, out_grad_ref, gates_ref, attended_ref, *out_refs
):
    me = place_ref[2]
    gate_ref = out_refs[0]
    slot_count, width = gate_ref.shape[1:]
    for step in range(group_count):
        group = (me if permuted else 0) ^ step
        attended = attended_ref[group].astype(jnp.float32)
        out_grad = out_grad_ref[group].astype(jnp.float32)
        center = attended - jnp.sum(attended, axis=1, keepdims=True) / width
        spread = jnp.sum(center * center, axis=1, keepdims=True) / width
        inverse = lax.rsqrt(spread + 1e-05)
        row_ids = lax.broadcasted_iota(jnp.int32, (slot_count, width), 0)
        gate_ref[group] = jnp.where(
            row_ids < plan_ref[group, me], out_grad * (center * inverse), 0.0
        ).astype(gate_ref.dtype)
        cotangent = out_grad * gates_ref[group].astype(jnp.float32)
        along = jnp.sum(cotangent * center, axis=1, keepdims=True)
        slope = along * (-1.0 / width) * (inverse * inverse * inverse)
        raw = cotangent * inverse + center * slope
        result = (raw - jnp.sum(raw, axis=1, keepdims=True) / width).astype(jnp.bfloat16)
        if permuted:
            out_refs[1 + step][:slot_count, :] = result
            if out_refs[1 + step].shape[0] > slot_count:
                out_refs[1 + step][slot_count:, :] = jnp.zeros(
                    (out_refs[1 + step].shape[0] - slot_count, width), jnp.bfloat16
                )
        else:
            out_refs[1][step] = result


def unpack_kernel(shape, permuted, place_ref, plan_ref, *refs):
    group_count, piece_count, _, slot_pad = shape
    block_refs, out_refs, (rows_ref,) = (
        refs[: -piece_count - 1],
        refs[-piece_count - 1 : -1],
        refs[-1:],
    )
    me, mine = place_ref[0], place_ref[2]
    rows, width = out_refs[0].shape
    if permuted:
        for step, block_ref in enumerate(block_refs):
            rows_ref[step * slot_pad : (step + 1) * slot_pad, :] = block_ref[...]
        source = rows_ref
    else:
        (source,) = block_refs
    select = select_matrix(
        lambda group: plan_ref[mine, group],
        mine if permuted else 0,
        group_count,
        source.shape[0] // group_count,
        rows,
    )
    for step, out_ref in enumerate(out_refs):
        out_ref[...] = jnp.dot(
            select, source[:, aligned(me ^ step, width)], preferred_element_type=jnp.float32
        ).astype(out_ref.dtype)


def pack_kernel(shape, permuted, place_ref, plan_ref, *refs):
    group_count, piece_count, _, slot_pad = shape
    block_refs, out_refs = refs[:piece_count], refs[piece_count:]
    me, mine = place_ref[0], place_ref[2]
    rows, width = block_refs[0].shape
    pad = slot_pad if permuted else out_refs[0].shape[0] // group_count
    select = select_matrix(
        lambda group: plan_ref[mine, group], mine if permuted else 0, group_count, pad, rows
    )
    for step, block_ref in enumerate(block_refs):
        columns = aligned(me ^ step, width)
        slots = lax.dot_general(
            select, block_ref[...], TN, preferred_element_type=jnp.float32
        ).astype(jnp.bfloat16)
        if permuted:
            for group, out_ref in enumerate(out_refs):
                out_ref[:, columns] = slots[group * pad : (group + 1) * pad, :]
        else:
            out_refs[0][:, columns] = slots


def regroup_kernel(shape, place_ref, *refs):
    _, piece_count, _, slot_pad = shape
    block_refs, out_refs = refs[:piece_count], refs[piece_count:]
    mine = place_ref[2]
    for step, out_ref in enumerate(out_refs):
        for piece, block_ref in enumerate(block_refs):
            out_ref[piece * slot_pad : (piece + 1) * slot_pad, :] = block_ref[
                aligned(mine ^ step, slot_pad), :
            ]


def ungroup_kernel(shape, place_ref, *refs):
    group_count, _, _, slot_pad = shape
    block_refs, out_refs = refs[:group_count], refs[group_count:]
    mine = place_ref[2]
    for step, block_ref in enumerate(block_refs):
        for piece, out_ref in enumerate(out_refs):
            out_ref[aligned(mine ^ step, slot_pad), :] = block_ref[
                piece * slot_pad : (piece + 1) * slot_pad, :
            ]


def unpack_pieces_kernel(shape, place_ref, counts_ref, *refs):
    group_count, _, _, slot_pad = shape
    block_refs = refs[:group_count]
    out_refs, rows_ref = refs[group_count:-1], refs[-1]
    rows = out_refs[0].shape[0]
    for piece, out_ref in enumerate(out_refs):
        for step, block_ref in enumerate(block_refs):
            rows_ref[piece, step * slot_pad : (step + 1) * slot_pad, :] = block_ref[
                piece * slot_pad : (piece + 1) * slot_pad, :
            ]
        select = select_matrix(
            lambda group, piece=piece: counts_ref[piece, group],
            place_ref[2],
            group_count,
            slot_pad,
            rows,
        )
        out_ref[...] = jnp.dot(
            select, rows_ref[piece], preferred_element_type=jnp.float32
        ).astype(out_ref.dtype)


def pack_pieces_kernel(shape, place_ref, counts_ref, *refs):
    group_count, piece_count, _, slot_pad = shape
    block_refs, out_refs = refs[:piece_count], refs[piece_count:]
    rows = block_refs[0].shape[0]
    for piece, block_ref in enumerate(block_refs):
        select = select_matrix(
            lambda group, piece=piece: counts_ref[piece, group],
            place_ref[2],
            group_count,
            slot_pad,
            rows,
        )
        slots = lax.dot_general(
            select, block_ref[...], TN, preferred_element_type=jnp.float32
        ).astype(jnp.bfloat16)
        for step, out_ref in enumerate(out_refs):
            out_ref[piece * slot_pad : (piece + 1) * slot_pad, :] = slots[
                step * slot_pad : (step + 1) * slot_pad, :
            ]


def place_kernel(place_ref, *refs):
    block_refs, out_ref, sems = refs[:-2], refs[-2], refs[-1]
    mine = place_ref[2]
    copies = [
        pltpu.make_async_copy(block_ref, out_ref.at[mine ^ step], sems.at[step])
        for step, block_ref in enumerate(block_refs)
    ]
    for copy in copies:
        copy.start()
    for copy in copies:
        copy.wait()


def join_kernel(place_ref, *refs):
    block_refs, out_ref, sems = refs[:-2], refs[-2], refs[-1]
    me = place_ref[0]
    width = block_refs[0].shape[1]
    copies = [
        pltpu.make_async_copy(
            block_ref, out_ref.at[:, aligned(me ^ step, width)], sems.at[step]
        )
        for step, block_ref in enumerate(block_refs)
    ]
    for copy in copies:
        copy.start()
    for copy in copies:
        copy.wait()


def gather_blocks(me, block_refs, scratch_ref):
    rows = block_refs[0].shape[0]
    for step, block_ref in enumerate(block_refs):
        scratch_ref[aligned(me ^ step, rows), :] = block_ref[...]


def spread_blocks(me, scratch_ref, out_refs):
    rows = out_refs[0].shape[0]
    for step, out_ref in enumerate(out_refs):
        out_ref[...] = scratch_ref[aligned(me ^ step, rows), :].astype(out_ref.dtype)


def live_tile(place_ref, mask_ref, inverse, query_start, key_start, rows):
    length = place_ref[1]
    row_ids = lax.broadcasted_iota(jnp.int32, (rows, rows), 0)
    column_ids = lax.broadcasted_iota(jnp.int32, (rows, rows), 1)
    key_pos = key_start + row_ids
    query_pos = query_start + column_ids
    blocks = rows // BLOCK
    allowed = jnp.zeros((rows, rows), jnp.int32)
    for key_sub in range(blocks):
        for query_sub in range(blocks):
            key_block = key_start // BLOCK + key_sub
            query_block = query_start // BLOCK + query_sub
            flag = jnp.where(key_block == query_block, 1, mask_ref[query_block, key_block])
            here = (row_ids // BLOCK == key_sub) & (column_ids // BLOCK == query_sub)
            allowed = jnp.where(here, flag, allowed)
    keep = (key_pos <= query_pos) & (query_pos < length) & (allowed > 0)
    return jnp.where(keep, inverse, 0.0)


def tile_of(query_piece, key_piece):
    return query_piece * (query_piece + 1) // 2 + key_piece


def tile_loop(pieces, body):
    def outer(query_piece, carry):
        def inner(key_piece, carry):
            body(query_piece, key_piece)
            return carry

        return lax.fori_loop(0, query_piece + 1, inner, carry)

    lax.fori_loop(0, pieces, outer, 0)


def weight_kernel(pieces, heads, place_ref, inverse_ref, mask_ref, *refs):
    query_refs, key_refs = refs[:pieces], refs[pieces : 2 * pieces]
    weight_ref, factor_ref, query_all, key_all = refs[2 * pieces :]
    me = place_ref[0]
    rows = query_refs[0].shape[0]
    size = query_all.shape[1] // heads
    gather_blocks(me, query_refs, query_all)
    gather_blocks(me, key_refs, key_all)
    inverse = inverse_ref[0]

    def body(query_piece, key_piece):
        query_start = query_piece * rows
        key_start = key_piece * rows
        live = live_tile(place_ref, mask_ref, inverse, query_start, key_start, rows)
        for head in range(heads):
            columns = pl.ds(head * size, size)
            scores = lax.dot_general(
                key_all[aligned(key_piece, rows), columns],
                query_all[aligned(query_piece, rows), columns],
                NT,
                preferred_element_type=jnp.float32,
            ) * (size ** (-0.5))
            sigmoid = 1.0 / (1.0 + jnp.exp(-scores))
            tile = tile_of(query_piece, key_piece)
            weight_ref[head, tile] = (scores * sigmoid * live).astype(weight_ref.dtype)
            factor_ref[head, tile] = sigmoid * (1.0 + scores * (1.0 - sigmoid)) * live

    tile_loop(pieces, body)


def value_kernel(pieces, heads, place_ref, weight_ref, *refs):
    grad_refs = refs[:pieces]
    out_refs = refs[pieces : 2 * pieces]
    grad_all, value_all = refs[2 * pieces :]
    me = place_ref[0]
    rows = grad_refs[0].shape[0]
    size = grad_all.shape[1] // heads
    gather_blocks(me, grad_refs, grad_all)
    for head in range(heads):
        columns = slice(head * size, (head + 1) * size)
        for key_piece in range(pieces):
            total = None
            for query_piece in range(key_piece, pieces):
                part = jnp.dot(
                    weight_ref[head, tile_of(query_piece, key_piece)],
                    grad_all[query_piece * rows : (query_piece + 1) * rows, columns],
                    preferred_element_type=jnp.float32,
                )
                total = part if total is None else total + part
            value_all[key_piece * rows : (key_piece + 1) * rows, columns] = total
    spread_blocks(me, value_all, out_refs)


def score_kernel(pieces, heads, place_ref, factor_ref, *refs):
    groups = [refs[index * pieces : (index + 1) * pieces] for index in range(6)]
    query_all, key_all, value_all, grad_all, query_sum, key_sum = refs[6 * pieces :]
    me = place_ref[0]
    rows = groups[0][0].shape[0]
    size = query_all.shape[1] // heads
    scale = size ** (-0.5)
    for blocks, scratch in zip(groups[:4], (query_all, key_all, value_all, grad_all)):
        gather_blocks(me, blocks, scratch)
    query_sum[...] = jnp.zeros_like(query_sum)
    key_sum[...] = jnp.zeros_like(key_sum)

    def body(query_piece, key_piece):
        query_rows = aligned(query_piece, rows)
        key_rows = aligned(key_piece, rows)
        for head in range(heads):
            columns = pl.ds(head * size, size)
            products = lax.dot_general(
                value_all[key_rows, columns],
                grad_all[query_rows, columns],
                NT,
                preferred_element_type=jnp.float32,
            )
            score_grad = (products * factor_ref[head, tile_of(query_piece, key_piece)]).astype(
                jnp.bfloat16
            )
            key_sum[key_rows, columns] += (
                jnp.dot(score_grad, query_all[query_rows, columns], preferred_element_type=jnp.float32)
                * scale
            )
            query_sum[query_rows, columns] += (
                lax.dot_general(
                    score_grad, key_all[key_rows, columns], TN, preferred_element_type=jnp.float32
                )
                * scale
            )

    tile_loop(pieces, body)
    spread_blocks(me, query_sum, groups[4])
    spread_blocks(me, key_sum, groups[5])


def local(queries, keys, values, gates, attended, out_grad, plan, hist_len, block_mask):
    group_count = lax.axis_size("dp")
    piece_count = lax.axis_size("seq")
    capacity = queries.shape[2]
    model_width = queries.shape[3]
    slot_count = capacity // group_count
    slot_pad = -(-slot_count // TILE) * TILE
    row_count = ROWS
    head_per = HEADS // piece_count
    width = model_width // piece_count
    full_len = row_count * piece_count
    tile_count = piece_count * (piece_count + 1) // 2
    shape = (group_count, piece_count, slot_count, slot_pad)
    dp_index = lax.axis_index("dp").astype(jnp.int32)
    length = hist_len[0]
    place = jnp.stack([lax.axis_index("seq").astype(jnp.int32), length, dp_index])
    inverse = (1.0 / jnp.sqrt(length.astype(jnp.float32))).reshape(1)
    mask = block_mask[0]
    my_plan = plan[:, 0, :]

    def like(*dims, dtype=jnp.bfloat16):
        return jax.ShapeDtypeStruct(dims, dtype)

    def by_slots(array):
        grouped = array.reshape(group_count, slot_count, model_width)
        if slot_pad > slot_count:
            grouped = jnp.pad(grouped, ((0, 0), (0, slot_pad - slot_count), (0, 0)))
        return grouped

    def exchange(blocks, axis):
        result = [blocks[0]]
        for step in range(1, len(blocks)):
            pairs = [(source, source ^ step) for source in range(len(blocks))]
            result.append(lax.ppermute(blocks[step], axis, pairs))
        return result

    def over_seq(blocks):
        return exchange(blocks, "seq")

    def over_dp(blocks, name):
        if name not in WHOLE:
            return exchange(blocks, "dp")
        (block,) = blocks
        return [
            lax.all_to_all(
                block.reshape(group_count, -1, model_width),
                "dp",
                split_axis=0,
                concat_axis=0,
                tiled=True,
            )
        ]

    def slot_blocks(array, name):
        if name in WHOLE:
            return [array.reshape(group_count, slot_count, model_width)]
        grouped = by_slots(array)
        return [
            lax.dynamic_index_in_dim(grouped, dp_index ^ step, 0, keepdims=False)
            for step in range(group_count)
        ]

    def to_history(blocks, name):
        blocks = over_dp(blocks, name)
        if name in WHOLE:
            blocks = [blocks[0].reshape(capacity, model_width)]
        return over_seq(
            call(
                functools.partial(unpack_kernel, shape, name not in WHOLE),
                [place, my_plan] + blocks,
                [like(row_count, width)] * piece_count,
                [pltpu.VMEM((group_count * slot_pad, model_width), jnp.bfloat16)],
                scalars=2,
            ),
        )

    def from_history(blocks, name):
        blocks = over_seq(blocks)
        whole = name in WHOLE
        blocks = call(
            functools.partial(pack_kernel, shape, not whole),
            [place, my_plan] + blocks,
            [like(capacity, model_width)] if whole else [like(slot_pad, model_width)] * group_count,
            scalars=2,
        )
        return over_dp(blocks, name)

    def placed(blocks, name):
        if name in WHOLE:
            return blocks[0]
        (result,) = call(
            place_kernel,
            [place] + blocks,
            [like(group_count, slot_pad, model_width)],
            [pltpu.SemaphoreType.DMA((group_count,))],
            scalars=1,
            any_space=True,
        )
        return result[:, :slot_count]

    plan_rows = jnp.zeros((TILE, width), jnp.bfloat16)
    own_counts = lax.dynamic_index_in_dim(my_plan, dp_index, 0, keepdims=True)
    plan_rows = lax.dynamic_update_slice(plan_rows, own_counts.astype(jnp.bfloat16), (0, 0))
    padded = group_count * slot_pad
    key_pieces = over_seq(
        call(
            split_kernel,
            [place, by_slots(keys).reshape(padded, model_width), plan_rows],
            [like(padded + TILE, width)] * piece_count,
            scalars=1,
        ),
    )

    permuted = "g" not in WHOLE
    grouped = (group_count, slot_count, model_width)
    gate_grad, *grad_slots = call(
        functools.partial(norm_kernel, group_count, permuted),
        [place, my_plan] + [array.reshape(grouped) for array in (out_grad, gates, attended)],
        [like(*grouped)]
        + ([like(slot_pad, model_width)] * group_count if permuted else [like(*grouped)]),
        scalars=2,
    )

    query_blocks = to_history(slot_blocks(queries, "q"), "q")
    value_blocks = to_history(slot_blocks(values, "v"), "v")
    grad_blocks = to_history(grad_slots, "g")

    counts = jnp.concatenate(
        [piece[padded : padded + 1, :group_count] for piece in key_pieces], axis=0
    ).astype(jnp.int32)
    key_groups = over_dp(
        call(
            functools.partial(regroup_kernel, shape),
            [place] + key_pieces,
            [like(piece_count * slot_pad, width)] * group_count,
            scalars=1,
        ),
        "k",
    )
    key_blocks = call(
        functools.partial(unpack_pieces_kernel, shape),
        [place, counts] + key_groups,
        [like(row_count, width)] * piece_count,
        [pltpu.VMEM((piece_count, padded, width), jnp.bfloat16)],
        scalars=2,
    )

    all_bf16 = pltpu.VMEM((full_len, width), jnp.bfloat16)
    all_f32 = pltpu.VMEM((full_len, width), jnp.float32)
    tiles = (head_per, tile_count, row_count, row_count)
    weight, factor = call(
        functools.partial(weight_kernel, piece_count, head_per),
        [place, inverse, mask] + query_blocks + key_blocks,
        [like(*tiles), like(*tiles, dtype=jnp.float32)],
        [all_bf16] * 2,
        scalars=3,
    )
    value_grads = call(
        functools.partial(value_kernel, piece_count, head_per),
        [place, weight] + grad_blocks,
        [like(row_count, width)] * piece_count,
        [all_bf16, all_f32],
        scalars=1,
    )
    score_grads = call(
        functools.partial(score_kernel, piece_count, head_per),
        [place, factor] + query_blocks + key_blocks + value_blocks + grad_blocks,
        [like(row_count, width)] * (2 * piece_count),
        [all_bf16] * 4 + [all_f32] * 2,
        scalars=1,
    )

    key_groups = over_dp(
        call(
            functools.partial(pack_pieces_kernel, shape),
            [place, counts] + score_grads[piece_count:],
            [like(piece_count * slot_pad, width)] * group_count,
            scalars=2,
        ),
        "dk",
    )
    value_out = from_history(value_grads, "dv")
    query_out = from_history(score_grads[:piece_count], "dq")
    key_pieces = over_seq(
        call(
            functools.partial(ungroup_kernel, shape),
            [place] + key_groups,
            [like(padded, width)] * piece_count,
            scalars=1,
        ),
    )
    (key_out,) = call(
        join_kernel,
        [place] + key_pieces,
        [like(padded, model_width)],
        [pltpu.SemaphoreType.DMA((piece_count,))],
        scalars=1,
        any_space=True,
    )
    key_out = key_out.reshape(group_count, slot_pad, model_width)[:, :slot_count]
    out_shape = (1, 1, capacity, model_width)
    return (
        placed(query_out, "dq").reshape(out_shape),
        key_out.reshape(out_shape),
        placed(value_out, "dv").reshape(out_shape),
        gate_grad.reshape(out_shape),
    )


def solution(mesh):
    rows_spec = P("dp", "seq", None, None)
    in_specs = (rows_spec,) * 6 + (P(None, "seq", None), P("dp"), P("dp", None, None))
    return jax.shard_map(
        local, mesh=mesh, in_specs=in_specs, out_specs=(rows_spec,) * 4, check_vma=False
    )
```

```python
import functools

import jax
import jax.numpy as jnp
from jax import lax
from jax.experimental import pallas as pl
from jax.experimental.pallas import tpu as pltpu
from jax.sharding import PartitionSpec as P


HEADS = 8
ROWS = 256
BLOCK = 128
TILE = 16

FIELDS = 3


WHOLE = ("q", "g", "dv")

VMEM_SPEC = pl.BlockSpec(memory_space=pltpu.VMEM)
SMEM_SPEC = pl.BlockSpec(memory_space=pltpu.SMEM)
HBM_SPEC = pl.BlockSpec(memory_space=pltpu.HBM)
NT = (((1,), (1,)), ((), ()))
TN = (((0,), (0,)), ((), ()))


def size_of(array):
    return array.size * array.dtype.itemsize


def call(kernel, inputs, outputs, scratch=(), scalars=0, far_in=0, far_out=0):
    in_specs = [SMEM_SPEC] * scalars + [HBM_SPEC] * far_in
    in_specs += [VMEM_SPEC] * (len(inputs) - len(in_specs))
    out_specs = [HBM_SPEC] * far_out + [VMEM_SPEC] * (len(outputs) - far_out)
    held = sum(size_of(array) for array in inputs[scalars + far_in :])
    held += sum(size_of(array) for array in outputs[far_out:])
    for ref in scratch:
        if ref.memory_space == pltpu.VMEM:
            held += ref.inner_aval.size * ref.inner_aval.dtype.itemsize
    inputs = [
        pltpu.with_memory_space_constraint(array, pltpu.HBM)
        if scalars <= index < scalars + far_in
        else array
        for index, array in enumerate(inputs)
    ]
    results = pl.pallas_call(
        kernel,
        out_shape=outputs,
        in_specs=in_specs,
        out_specs=out_specs,
        scratch_shapes=list(scratch),
        compiler_params=pltpu.CompilerParams(vmem_limit_bytes=held + (6 << 20)),
    )(*inputs)
    return list(results)


def run_copies(pairs, sems):
    copies = [
        pltpu.make_async_copy(source, target, sems.at[index])
        for index, (source, target) in enumerate(pairs)
    ]
    for copy in copies:
        copy.start()
    return copies


def wait_all(copies):
    for copy in copies:
        copy.wait()


def aligned(index, size):
    return pl.ds(pl.multiple_of(index * size, size), size)


def select_matrix(count_at, mixed, group_count, slot_pad, rows):
    capacity = group_count * slot_pad
    lanes = lax.broadcasted_iota(jnp.int32, (1, capacity), 1)
    before = []
    total = jnp.int32(0)
    for group in range(group_count):
        before.append(total)
        total = total + count_at(jnp.int32(group))
    slot_rows = jnp.full((1, capacity), -1, jnp.int32)
    for place in range(group_count):
        group = mixed ^ place
        start = jnp.int32(0)
        for other in range(group_count):
            start = jnp.where(group == other, before[other], start)
        slot = lanes - place * slot_pad
        inside = (slot >= 0) & (slot < count_at(group))
        slot_rows = jnp.where(inside, start + slot, slot_rows)
    row_ids = lax.broadcasted_iota(jnp.int32, (rows, capacity), 0)
    return (row_ids == slot_rows).astype(jnp.float32).astype(jnp.bfloat16)


def split_kernel(group_count, place_ref, rows_ref, *refs):
    out_refs, sems = refs[:-1], refs[-1]
    me = place_ref[0]
    capacity = rows_ref.shape[0]
    width = out_refs[0].shape[1]
    copies = run_copies(
        [
            (rows_ref.at[:, aligned(me ^ step, width)], out_ref.at[:capacity])
            for step, out_ref in enumerate(out_refs)
        ],
        sems,
    )
    lanes = lax.broadcasted_iota(jnp.int32, (TILE, width), 1)
    counts = jnp.zeros((TILE, width), jnp.int32)
    for group in range(group_count):
        counts = jnp.where(lanes == group, place_ref[FIELDS + group], counts)
    counts = counts.astype(jnp.float32).astype(jnp.bfloat16)
    for out_ref in out_refs:
        out_ref[capacity:, :] = counts
    wait_all(copies)


def slots_kernel(place_ref, slots_ref, *refs):
    out_refs, sems = refs[:-1], refs[-1]
    mine = place_ref[2]
    wait_all(
        run_copies(
            [(slots_ref.at[mine ^ step], out_ref) for step, out_ref in enumerate(out_refs)], sems
        )
    )


def norm_kernel(group_count, place_ref, *refs):
    far_refs, (gate_ref, grad_ref, held_ref, made_ref, sems, out_sems) = refs[:3], refs[3:]
    slot_count, width = grad_ref.shape[1:]
    half = group_count // 2
    parts = [slice(0, half), slice(half, group_count)]
    loads = [
        run_copies(
            [(far_ref.at[part], held_ref.at[index, part]) for index, far_ref in enumerate(far_refs)],
            sems.at[place],
        )
        for place, part in enumerate(parts)
    ]
    stores = []
    row_ids = lax.broadcasted_iota(jnp.int32, (slot_count, width), 0)
    for place, part in enumerate(parts):
        wait_all(loads[place])
        for group in range(part.start, part.stop):
            out_grad = held_ref[0, group].astype(jnp.float32)
            gates = held_ref[1, group].astype(jnp.float32)
            attended = held_ref[2, group].astype(jnp.float32)
            center = attended - jnp.sum(attended, axis=1, keepdims=True) / width
            spread = jnp.sum(center * center, axis=1, keepdims=True) / width
            inverse = lax.rsqrt(spread + 1e-05)
            made_ref[group] = jnp.where(
                row_ids < place_ref[FIELDS + group_count + group],
                out_grad * (center * inverse),
                0.0,
            ).astype(made_ref.dtype)
            cotangent = out_grad * gates
            along = jnp.sum(cotangent * center, axis=1, keepdims=True)
            slope = along * (-1.0 / width) * (inverse * inverse * inverse)
            raw = cotangent * inverse + center * slope
            grad_ref[group] = (raw - jnp.sum(raw, axis=1, keepdims=True) / width).astype(
                grad_ref.dtype
            )
        stores += run_copies([(made_ref.at[part], gate_ref.at[part])], out_sems.at[place])
    wait_all(stores)


def unpack_kernel(shape, permuted, place_ref, *refs):
    group_count, piece_count, _, slot_pad = shape
    block_refs, out_refs, (rows_ref,) = (
        refs[: -piece_count - 1],
        refs[-piece_count - 1 : -1],
        refs[-1:],
    )
    me, mine = place_ref[0], place_ref[2]
    rows, width = out_refs[0].shape
    if permuted:
        for step, block_ref in enumerate(block_refs):
            rows_ref[step * slot_pad : (step + 1) * slot_pad, :] = block_ref[...]
        source = rows_ref
    else:
        (source,) = block_refs
    select = select_matrix(
        lambda group: place_ref[FIELDS + group],
        mine if permuted else 0,
        group_count,
        source.shape[0] // group_count,
        rows,
    )
    for step, out_ref in enumerate(out_refs):
        out_ref[...] = jnp.dot(
            select, source[:, aligned(me ^ step, width)], preferred_element_type=jnp.float32
        ).astype(out_ref.dtype)


def pack_kernel(shape, permuted, place_ref, *refs):
    group_count, piece_count, _, slot_pad = shape
    block_refs, out_refs = refs[:piece_count], refs[piece_count:]
    me, mine = place_ref[0], place_ref[2]
    rows, width = block_refs[0].shape
    pad = slot_pad if permuted else out_refs[0].shape[0] // group_count
    select = select_matrix(
        lambda group: place_ref[FIELDS + group], mine if permuted else 0, group_count, pad, rows
    )
    for step, block_ref in enumerate(block_refs):
        columns = aligned(me ^ step, width)
        slots = lax.dot_general(
            select, block_ref[...], TN, preferred_element_type=jnp.float32
        ).astype(jnp.bfloat16)
        if permuted:
            for group, out_ref in enumerate(out_refs):
                out_ref[:, columns] = slots[group * pad : (group + 1) * pad, :]
        else:
            out_refs[0][:, columns] = slots


def regroup_kernel(shape, place_ref, *refs):
    _, piece_count, _, slot_pad = shape
    block_refs, out_refs = refs[:piece_count], refs[piece_count:]
    mine = place_ref[2]
    for step, out_ref in enumerate(out_refs):
        for piece, block_ref in enumerate(block_refs):
            out_ref[piece * slot_pad : (piece + 1) * slot_pad, :] = block_ref[
                aligned(mine ^ step, slot_pad), :
            ]


def ungroup_kernel(shape, place_ref, *refs):
    group_count, _, _, slot_pad = shape
    block_refs, out_refs = refs[:group_count], refs[group_count:]
    mine = place_ref[2]
    for step, block_ref in enumerate(block_refs):
        for piece, out_ref in enumerate(out_refs):
            out_ref[aligned(mine ^ step, slot_pad), :] = block_ref[
                piece * slot_pad : (piece + 1) * slot_pad, :
            ]


def unpack_pieces_kernel(shape, place_ref, counts_ref, *refs):
    group_count, _, _, slot_pad = shape
    block_refs = refs[:group_count]
    out_refs, rows_ref = refs[group_count:-1], refs[-1]
    rows = out_refs[0].shape[0]
    for piece, out_ref in enumerate(out_refs):
        for step, block_ref in enumerate(block_refs):
            rows_ref[piece, step * slot_pad : (step + 1) * slot_pad, :] = block_ref[
                piece * slot_pad : (piece + 1) * slot_pad, :
            ]
        select = select_matrix(
            lambda group, piece=piece: counts_ref[piece, group],
            place_ref[2],
            group_count,
            slot_pad,
            rows,
        )
        out_ref[...] = jnp.dot(
            select, rows_ref[piece], preferred_element_type=jnp.float32
        ).astype(out_ref.dtype)


def pack_pieces_kernel(shape, place_ref, counts_ref, *refs):
    group_count, piece_count, _, slot_pad = shape
    block_refs, out_refs = refs[:piece_count], refs[piece_count:]
    rows = block_refs[0].shape[0]
    for piece, block_ref in enumerate(block_refs):
        select = select_matrix(
            lambda group, piece=piece: counts_ref[piece, group],
            place_ref[2],
            group_count,
            slot_pad,
            rows,
        )
        slots = lax.dot_general(
            select, block_ref[...], TN, preferred_element_type=jnp.float32
        ).astype(jnp.bfloat16)
        for step, out_ref in enumerate(out_refs):
            out_ref[piece * slot_pad : (piece + 1) * slot_pad, :] = slots[
                step * slot_pad : (step + 1) * slot_pad, :
            ]


def place_kernel(block_ref, out_ref, sems):
    wait_all(run_copies([(block_ref, out_ref)], sems))


def finish_kernel(shape, whole, place_ref, *refs):
    _, piece_count, _, _ = shape
    sems = refs[-1]
    key_refs, query_refs = refs[:piece_count], refs[piece_count:-3]
    query_out, key_out = refs[-3:-1]
    me, mine = place_ref[0], place_ref[2]
    width = key_refs[0].shape[1]
    if whole:
        pairs = [(query_refs[0], query_out)]
    else:
        pairs = [
            (query_ref, query_out.at[mine ^ step]) for step, query_ref in enumerate(query_refs)
        ]
    pairs += [
        (key_ref, key_out.at[:, aligned(me ^ step, width)]) for step, key_ref in enumerate(key_refs)
    ]
    wait_all(run_copies(pairs, sems))


def gather_blocks(me, block_refs, scratch_ref):
    rows = block_refs[0].shape[0]
    for step, block_ref in enumerate(block_refs):
        scratch_ref[aligned(me ^ step, rows), :] = block_ref[...]


def spread_blocks(me, scratch_ref, out_refs):
    rows = out_refs[0].shape[0]
    for step, out_ref in enumerate(out_refs):
        out_ref[...] = scratch_ref[aligned(me ^ step, rows), :].astype(out_ref.dtype)


def live_tile(place_ref, mask_ref, inverse, query_start, key_start, rows):
    length = place_ref[1]
    row_ids = lax.broadcasted_iota(jnp.int32, (rows, rows), 0)
    column_ids = lax.broadcasted_iota(jnp.int32, (rows, rows), 1)
    key_pos = key_start + row_ids
    query_pos = query_start + column_ids
    blocks = rows // BLOCK
    allowed = jnp.zeros((rows, rows), jnp.int32)
    for key_sub in range(blocks):
        for query_sub in range(blocks):
            key_block = key_start // BLOCK + key_sub
            query_block = query_start // BLOCK + query_sub
            flag = jnp.where(key_block == query_block, 1, mask_ref[query_block, key_block])
            here = (row_ids // BLOCK == key_sub) & (column_ids // BLOCK == query_sub)
            allowed = jnp.where(here, flag, allowed)
    keep = (key_pos <= query_pos) & (query_pos < length) & (allowed > 0)
    return jnp.where(keep, inverse, 0.0)


def tile_of(query_piece, key_piece):
    return query_piece * (query_piece + 1) // 2 + key_piece


def tile_loop(pieces, body):
    def outer(query_piece, carry):
        def inner(key_piece, carry):
            body(query_piece, key_piece)
            return carry

        return lax.fori_loop(0, query_piece + 1, inner, carry)

    lax.fori_loop(0, pieces, outer, 0)


def weight_kernel(pieces, heads, place_ref, inverse_ref, mask_ref, *refs):
    query_refs, key_refs = refs[:pieces], refs[pieces : 2 * pieces]
    weight_ref, factor_ref, query_all, key_all = refs[2 * pieces :]
    me = place_ref[0]
    rows = query_refs[0].shape[0]
    size = query_all.shape[1] // heads
    gather_blocks(me, query_refs, query_all)
    gather_blocks(me, key_refs, key_all)
    inverse = inverse_ref[0]

    def body(query_piece, key_piece):
        query_start = query_piece * rows
        key_start = key_piece * rows
        live = live_tile(place_ref, mask_ref, inverse, query_start, key_start, rows)
        for head in range(heads):
            columns = pl.ds(head * size, size)
            scores = lax.dot_general(
                key_all[aligned(key_piece, rows), columns],
                query_all[aligned(query_piece, rows), columns],
                NT,
                preferred_element_type=jnp.float32,
            ) * (size ** (-0.5))
            sigmoid = 1.0 / (1.0 + jnp.exp(-scores))
            tile = tile_of(query_piece, key_piece)
            weight_ref[head, tile] = (scores * sigmoid * live).astype(weight_ref.dtype)
            factor_ref[head, tile] = sigmoid * (1.0 + scores * (1.0 - sigmoid)) * live

    tile_loop(pieces, body)


def value_kernel(pieces, heads, place_ref, weight_ref, *refs):
    grad_refs = refs[:pieces]
    out_refs = refs[pieces : 2 * pieces]
    grad_all, value_all = refs[2 * pieces :]
    me = place_ref[0]
    rows = grad_refs[0].shape[0]
    size = grad_all.shape[1] // heads
    gather_blocks(me, grad_refs, grad_all)
    for head in range(heads):
        columns = slice(head * size, (head + 1) * size)
        for key_piece in range(pieces):
            total = None
            for query_piece in range(key_piece, pieces):
                part = jnp.dot(
                    weight_ref[head, tile_of(query_piece, key_piece)],
                    grad_all[query_piece * rows : (query_piece + 1) * rows, columns],
                    preferred_element_type=jnp.float32,
                )
                total = part if total is None else total + part
            value_all[key_piece * rows : (key_piece + 1) * rows, columns] = total
    spread_blocks(me, value_all, out_refs)


def score_kernel(pieces, heads, place_ref, factor_ref, *refs):
    groups = [refs[index * pieces : (index + 1) * pieces] for index in range(6)]
    query_all, key_all, value_all, grad_all, query_sum, key_sum, held = refs[6 * pieces :]
    me = place_ref[0]
    rows = groups[0][0].shape[0]
    size = query_all.shape[1] // heads
    scale = size ** (-0.5)
    for blocks, scratch in zip(groups[:4], (query_all, key_all, value_all, grad_all)):
        gather_blocks(me, blocks, scratch)

    def part(piece):
        return slice(piece * rows, (piece + 1) * rows)

    for head in range(heads):
        columns = slice(head * size, (head + 1) * size)
        for query_piece in range(pieces):
            total = None
            for key_piece in range(query_piece + 1):
                tile = tile_of(query_piece, key_piece)
                products = lax.dot_general(
                    value_all[part(key_piece), columns],
                    grad_all[part(query_piece), columns],
                    NT,
                    preferred_element_type=jnp.float32,
                )
                score_grad = (products * factor_ref[head, tile]).astype(jnp.bfloat16)
                held[head, tile] = score_grad
                term = lax.dot_general(
                    score_grad, key_all[part(key_piece), columns], TN, preferred_element_type=jnp.float32
                )
                total = term if total is None else total + term
            query_sum[part(query_piece), columns] = (total * scale).astype(jnp.bfloat16)
        for key_piece in range(pieces):
            total = None
            for query_piece in range(key_piece, pieces):
                term = jnp.dot(
                    held[head, tile_of(query_piece, key_piece)],
                    query_all[part(query_piece), columns],
                    preferred_element_type=jnp.float32,
                )
                total = term if total is None else total + term
            key_sum[part(key_piece), columns] = (total * scale).astype(jnp.bfloat16)
    spread_blocks(me, query_sum, groups[4])
    spread_blocks(me, key_sum, groups[5])


def local(queries, keys, values, gates, attended, out_grad, plan, hist_len, block_mask):
    group_count = lax.axis_size("dp")
    piece_count = lax.axis_size("seq")
    capacity = queries.shape[2]
    model_width = queries.shape[3]
    slot_count = capacity // group_count
    slot_pad = -(-slot_count // TILE) * TILE
    row_count = ROWS
    head_per = HEADS // piece_count
    width = model_width // piece_count
    full_len = row_count * piece_count
    tile_count = piece_count * (piece_count + 1) // 2
    shape = (group_count, piece_count, slot_count, slot_pad)
    dp_index = lax.axis_index("dp").astype(jnp.int32)
    length = hist_len[0]
    group_ids = jnp.arange(group_count, dtype=jnp.int32)
    my_plan = plan[:, 0, :]
    own_counts = jnp.sum(jnp.where(group_ids[:, None] == dp_index, my_plan, 0), axis=0)
    incoming = jnp.sum(jnp.where(group_ids[None, :] == dp_index, my_plan, 0), axis=1)
    fields = jnp.stack([lax.axis_index("seq").astype(jnp.int32), length, dp_index])
    place = jnp.concatenate([fields, own_counts, incoming])
    inverse = (1.0 / jnp.sqrt(length.astype(jnp.float32))).reshape(1)
    mask = block_mask[0]

    def like(*dims, dtype=jnp.bfloat16):
        return jax.ShapeDtypeStruct(dims, dtype)

    def by_slots(array):
        grouped = array.reshape(group_count, slot_count, model_width)
        if slot_pad > slot_count:
            grouped = jnp.pad(grouped, ((0, 0), (0, slot_pad - slot_count), (0, 0)))
        return grouped

    def exchange(blocks, axis):
        result = [blocks[0]]
        for step in range(1, len(blocks)):
            pairs = [(source, source ^ step) for source in range(len(blocks))]
            result.append(lax.ppermute(blocks[step], axis, pairs))
        return result

    def over_seq(blocks):
        return exchange(blocks, "seq")

    def over_dp(blocks, name):
        if name not in WHOLE:
            return exchange(blocks, "dp")
        (block,) = blocks
        return [
            lax.all_to_all(
                block.reshape(group_count, -1, model_width),
                "dp",
                split_axis=0,
                concat_axis=0,
                tiled=True,
            )
        ]

    def slot_blocks(array, name):
        if name in WHOLE:
            return [array.reshape(group_count, slot_count, model_width)]
        return call(
            slots_kernel,
            [place, by_slots(array)],
            [like(slot_pad, model_width)] * group_count,
            [pltpu.SemaphoreType.DMA((group_count,))],
            scalars=1,
            far_in=1,
        )

    def to_history(blocks, name):
        blocks = over_dp(blocks, name)
        if name in WHOLE:
            blocks = [blocks[0].reshape(capacity, model_width)]
        return over_seq(
            call(
                functools.partial(unpack_kernel, shape, name not in WHOLE),
                [place] + blocks,
                [like(row_count, width)] * piece_count,
                [pltpu.VMEM((group_count * slot_pad, model_width), jnp.bfloat16)],
                scalars=1,
            ),
        )

    def from_history(blocks, name):
        blocks = over_seq(blocks)
        whole = name in WHOLE
        blocks = call(
            functools.partial(pack_kernel, shape, not whole),
            [place] + blocks,
            [like(capacity, model_width)] if whole else [like(slot_pad, model_width)] * group_count,
            scalars=1,
        )
        return over_dp(blocks, name)

    padded = group_count * slot_pad
    key_pieces = over_seq(
        call(
            functools.partial(split_kernel, group_count),
            [place, by_slots(keys).reshape(padded, model_width)],
            [like(padded + TILE, width)] * piece_count,
            [pltpu.SemaphoreType.DMA((piece_count,))],
            scalars=1,
            far_in=1,
        ),
    )

    grouped = (group_count, slot_count, model_width)
    gate_grad, attn_grad = call(
        functools.partial(norm_kernel, group_count),
        [place] + [array.reshape(grouped) for array in (out_grad, gates, attended)],
        [like(*grouped)] * 2,
        [
            pltpu.VMEM((3,) + grouped, jnp.bfloat16),
            pltpu.VMEM(grouped, jnp.bfloat16),
            pltpu.SemaphoreType.DMA((2, 3)),
            pltpu.SemaphoreType.DMA((2, 1)),
        ],
        scalars=1,
        far_in=3,
        far_out=1,
    )

    query_blocks = to_history(slot_blocks(queries, "q"), "q")
    value_blocks = to_history(slot_blocks(values, "v"), "v")
    grad_blocks = to_history([attn_grad], "g")

    counts = jnp.concatenate(
        [piece[padded : padded + 1, :group_count] for piece in key_pieces], axis=0
    ).astype(jnp.int32)
    key_groups = over_dp(
        call(
            functools.partial(regroup_kernel, shape),
            [place] + key_pieces,
            [like(piece_count * slot_pad, width)] * group_count,
            scalars=1,
        ),
        "k",
    )
    key_blocks = call(
        functools.partial(unpack_pieces_kernel, shape),
        [place, counts] + key_groups,
        [like(row_count, width)] * piece_count,
        [pltpu.VMEM((piece_count, padded, width), jnp.bfloat16)],
        scalars=2,
    )

    all_bf16 = pltpu.VMEM((full_len, width), jnp.bfloat16)
    all_f32 = pltpu.VMEM((full_len, width), jnp.float32)
    tiles = (head_per, tile_count, row_count, row_count)
    weight, factor = call(
        functools.partial(weight_kernel, piece_count, head_per),
        [place, inverse, mask] + query_blocks + key_blocks,
        [like(*tiles), like(*tiles, dtype=jnp.float32)],
        [all_bf16] * 2,
        scalars=3,
    )
    value_grads = call(
        functools.partial(value_kernel, piece_count, head_per),
        [place, weight] + grad_blocks,
        [like(row_count, width)] * piece_count,
        [all_bf16, all_f32],
        scalars=1,
    )
    score_grads = call(
        functools.partial(score_kernel, piece_count, head_per),
        [place, factor] + query_blocks + key_blocks + value_blocks + grad_blocks,
        [like(row_count, width)] * (2 * piece_count),
        [all_bf16] * 6 + [pltpu.VMEM(tiles, jnp.bfloat16)],
        scalars=1,
    )

    key_groups = over_dp(
        call(
            functools.partial(pack_pieces_kernel, shape),
            [place, counts] + score_grads[piece_count:],
            [like(piece_count * slot_pad, width)] * group_count,
            scalars=2,
        ),
        "dk",
    )
    value_out = from_history(value_grads, "dv")
    query_out = from_history(score_grads[:piece_count], "dq")
    key_pieces = over_seq(
        call(
            functools.partial(ungroup_kernel, shape),
            [place] + key_groups,
            [like(padded, width)] * piece_count,
            scalars=1,
        ),
    )
    (value_out,) = call(
        place_kernel,
        value_out,
        [like(*value_out[0].shape)],
        [pltpu.SemaphoreType.DMA((1,))],
        far_out=1,
    )
    whole = "dq" in WHOLE
    query_out, key_out = call(
        functools.partial(finish_kernel, shape, whole),
        [place] + key_pieces + query_out,
        [
            like(group_count, slot_count if whole else slot_pad, model_width),
            like(padded, model_width),
        ],
        [pltpu.SemaphoreType.DMA((group_count + piece_count,))],
        scalars=1,
        far_out=2,
    )
    key_out = key_out.reshape(group_count, slot_pad, model_width)
    out_shape = (1, 1, capacity, model_width)
    return (
        query_out[:, :slot_count].reshape(out_shape),
        key_out[:, :slot_count].reshape(out_shape),
        value_out.reshape(out_shape),
        gate_grad.reshape(out_shape),
    )


def solution(mesh):
    rows_spec = P("dp", "seq", None, None)
    in_specs = (rows_spec,) * 6 + (P(None, "seq", None), P("dp"), P("dp", None, None))
    return jax.shard_map(
        local, mesh=mesh, in_specs=in_specs, out_specs=(rows_spec,) * 4, check_vma=False
    )
```

```python
import functools

import jax
import jax.numpy as jnp
from jax import lax
from jax.experimental import pallas as pl
from jax.experimental.pallas import tpu as pltpu
from jax.sharding import PartitionSpec as P


HEADS = 8
ROWS = 256
BLOCK = 128
TILE = 16

FIELDS = 3

CUTS = 4

PARTS = 2


WHOLE = ("q", "g", "dv")

VMEM_SPEC = pl.BlockSpec(memory_space=pltpu.VMEM)
SMEM_SPEC = pl.BlockSpec(memory_space=pltpu.SMEM)
HBM_SPEC = pl.BlockSpec(memory_space=pltpu.HBM)
NT = (((1,), (1,)), ((), ()))
TN = (((0,), (0,)), ((), ()))


def size_of(array):
    return array.size * array.dtype.itemsize


def call(kernel, inputs, outputs, scratch=(), scalars=0, far_in=0, far_out=0, scalar_out=0):
    in_specs = [SMEM_SPEC] * scalars + [HBM_SPEC] * far_in
    in_specs += [VMEM_SPEC] * (len(inputs) - len(in_specs))
    out_specs = [HBM_SPEC] * far_out + [VMEM_SPEC] * (len(outputs) - far_out - scalar_out)
    out_specs += [SMEM_SPEC] * scalar_out
    held = sum(size_of(array) for array in inputs[scalars + far_in :])
    held += sum(size_of(array) for array in outputs[far_out:])
    for ref in scratch:
        if ref.memory_space == pltpu.VMEM:
            held += ref.inner_aval.size * ref.inner_aval.dtype.itemsize
    inputs = [
        pltpu.with_memory_space_constraint(array, pltpu.HBM)
        if scalars <= index < scalars + far_in
        else array
        for index, array in enumerate(inputs)
    ]
    results = pl.pallas_call(
        kernel,
        out_shape=outputs,
        in_specs=in_specs,
        out_specs=out_specs,
        scratch_shapes=list(scratch),
        compiler_params=pltpu.CompilerParams(vmem_limit_bytes=held + (6 << 20)),
    )(*inputs)
    return list(results)


def run_copies(pairs, sems):
    copies = [
        pltpu.make_async_copy(source, target, sems.at[index])
        for index, (source, target) in enumerate(pairs)
    ]
    for copy in copies:
        copy.start()
    return copies


def wait_all(copies):
    for copy in copies:
        copy.wait()


def aligned(index, size):
    return pl.ds(pl.multiple_of(index * size, size), size)


def select_matrix(count_at, mixed, group_count, slot_pad, rows):
    capacity = group_count * slot_pad
    lanes = lax.broadcasted_iota(jnp.int32, (1, capacity), 1)
    before = []
    total = jnp.int32(0)
    for group in range(group_count):
        before.append(total)
        total = total + count_at(jnp.int32(group))
    slot_rows = jnp.full((1, capacity), -1, jnp.int32)
    for place in range(group_count):
        group = mixed ^ place
        start = jnp.int32(0)
        for other in range(group_count):
            start = jnp.where(group == other, before[other], start)
        slot = lanes - place * slot_pad
        inside = (slot >= 0) & (slot < count_at(group))
        slot_rows = jnp.where(inside, start + slot, slot_rows)
    row_ids = lax.broadcasted_iota(jnp.int32, (rows, capacity), 0)
    return (row_ids == slot_rows).astype(jnp.float32).astype(jnp.bfloat16)


def split_kernel(group_count, length_ref, rows_ref, plan_ref, *refs):
    out_refs, (place_ref, plan_held, rows_held, sems, plan_sem) = refs[:-5], refs[-5:]
    me = lax.axis_index("seq").astype(jnp.int32)
    mine = lax.axis_index("dp").astype(jnp.int32)
    capacity = rows_ref.shape[0]
    width = out_refs[0].shape[1]
    plan_copy = pltpu.make_async_copy(plan_ref, plan_held, plan_sem.at[0])
    plan_copy.start()
    cut = capacity // CUTS
    parts = [slice(index * cut, (index + 1) * cut) for index in range(CUTS)]
    copies = run_copies([(rows_ref.at[part], rows_held.at[part]) for part in parts], sems)
    plan_copy.wait()
    place_ref[0] = me
    place_ref[1] = length_ref[0]
    place_ref[2] = mine
    lanes = lax.broadcasted_iota(jnp.int32, (TILE, width), 1)
    counts = jnp.zeros((TILE, width), jnp.int32)
    for group in range(group_count):
        count = plan_held[mine, 0, group]
        place_ref[FIELDS + group] = count
        place_ref[FIELDS + group_count + group] = plan_held[group, 0, mine]
        counts = jnp.where(lanes == group, count, counts)
    counts = counts.astype(jnp.float32).astype(jnp.bfloat16)
    for out_ref in out_refs:
        out_ref[capacity:, :] = counts
    for part, copy in zip(parts, copies):
        copy.wait()
        for step, out_ref in enumerate(out_refs):
            out_ref[part, :] = rows_held[part, aligned(me ^ step, width)]


def norm_kernel(group_count, place_ref, *refs):
    far_refs, slots_ref, out_refs, slot_refs = refs[:3], refs[3], refs[4:6], refs[6:-5]
    held_ref, made_ref, sems, out_sems, slot_sems = refs[-5:]
    slot_count, width = made_ref.shape[2:]
    half = group_count // PARTS
    parts = [slice(index * half, (index + 1) * half) for index in range(PARTS)]
    loads = [
        run_copies(
            [(far_ref.at[part], held_ref.at[index, part]) for index, far_ref in enumerate(far_refs)],
            sems.at[place],
        )
        for place, part in enumerate(parts)
    ]
    mine = place_ref[2]
    stores = run_copies(
        [(slots_ref.at[mine ^ step], slot_ref) for step, slot_ref in enumerate(slot_refs)],
        slot_sems,
    )
    row_ids = lax.broadcasted_iota(jnp.int32, (slot_count, width), 0)
    for place, part in enumerate(parts):
        wait_all(loads[place])
        for group in range(part.start, part.stop):
            out_grad = held_ref[0, group].astype(jnp.float32)
            gates = held_ref[1, group].astype(jnp.float32)
            attended = held_ref[2, group].astype(jnp.float32)
            center = attended - jnp.sum(attended, axis=1, keepdims=True) / width
            spread = jnp.sum(center * center, axis=1, keepdims=True) / width
            inverse = lax.rsqrt(spread + 1e-05)
            made_ref[0, group] = jnp.where(
                row_ids < place_ref[FIELDS + group_count + group],
                out_grad * (center * inverse),
                0.0,
            ).astype(made_ref.dtype)
            cotangent = out_grad * gates
            along = jnp.sum(cotangent * center, axis=1, keepdims=True)
            slope = along * (-1.0 / width) * (inverse * inverse * inverse)
            raw = cotangent * inverse + center * slope
            made_ref[1, group] = (raw - jnp.sum(raw, axis=1, keepdims=True) / width).astype(
                made_ref.dtype
            )
        stores += run_copies(
            [(made_ref.at[index, part], out_ref.at[part]) for index, out_ref in enumerate(out_refs)],
            out_sems.at[place],
        )
    wait_all(stores)


def unpack_kernel(shape, permuted, place_ref, *refs):
    group_count, piece_count, _, slot_pad = shape
    me, mine = place_ref[0], place_ref[2]
    block_refs, out_refs, rows_ref = refs[: -piece_count - 1], refs[-piece_count - 1 : -1], refs[-1]
    rows, width = out_refs[0].shape
    if permuted:
        for step, block_ref in enumerate(block_refs):
            rows_ref[step * slot_pad : (step + 1) * slot_pad, :] = block_ref[...]
        source = rows_ref
    else:
        (source,) = block_refs
    select = select_matrix(
        lambda group: place_ref[FIELDS + group],
        mine if permuted else 0,
        group_count,
        source.shape[0] // group_count,
        rows,
    )
    for step, out_ref in enumerate(out_refs):
        out_ref[...] = jnp.dot(
            select, source[:, aligned(me ^ step, width)], preferred_element_type=jnp.float32
        ).astype(out_ref.dtype)


def pack_kernel(shape, permuted, place_ref, *refs):
    group_count, piece_count, _, slot_pad = shape
    block_refs, out_refs = refs[:piece_count], refs[piece_count:]
    me, mine = place_ref[0], place_ref[2]
    rows, width = block_refs[0].shape
    pad = slot_pad if permuted else out_refs[0].shape[0] // group_count
    select = select_matrix(
        lambda group: place_ref[FIELDS + group], mine if permuted else 0, group_count, pad, rows
    )
    for step, block_ref in enumerate(block_refs):
        columns = aligned(me ^ step, width)
        slots = lax.dot_general(
            select, block_ref[...], TN, preferred_element_type=jnp.float32
        ).astype(jnp.bfloat16)
        if permuted:
            for group, out_ref in enumerate(out_refs):
                out_ref[:, columns] = slots[group * pad : (group + 1) * pad, :]
        else:
            out_refs[0][:, columns] = slots


def regroup_kernel(shape, place_ref, *refs):
    _, piece_count, _, slot_pad = shape
    block_refs, out_refs = refs[:piece_count], refs[piece_count:]
    mine = place_ref[2]
    for step, out_ref in enumerate(out_refs):
        for piece, block_ref in enumerate(block_refs):
            out_ref[piece * slot_pad : (piece + 1) * slot_pad, :] = block_ref[
                aligned(mine ^ step, slot_pad), :
            ]


def ungroup_kernel(shape, place_ref, *refs):
    group_count, _, _, slot_pad = shape
    block_refs, out_refs = refs[:group_count], refs[group_count:]
    mine = place_ref[2]
    for step, block_ref in enumerate(block_refs):
        for piece, out_ref in enumerate(out_refs):
            out_ref[aligned(mine ^ step, slot_pad), :] = block_ref[
                piece * slot_pad : (piece + 1) * slot_pad, :
            ]


def unpack_pieces_kernel(shape, place_ref, counts_ref, *refs):
    group_count, _, _, slot_pad = shape
    block_refs = refs[:group_count]
    out_refs, rows_ref = refs[group_count:-1], refs[-1]
    rows = out_refs[0].shape[0]
    for piece, out_ref in enumerate(out_refs):
        for step, block_ref in enumerate(block_refs):
            rows_ref[piece, step * slot_pad : (step + 1) * slot_pad, :] = block_ref[
                piece * slot_pad : (piece + 1) * slot_pad, :
            ]
        select = select_matrix(
            lambda group, piece=piece: counts_ref[piece, group],
            place_ref[2],
            group_count,
            slot_pad,
            rows,
        )
        out_ref[...] = jnp.dot(
            select, rows_ref[piece], preferred_element_type=jnp.float32
        ).astype(out_ref.dtype)


def pack_pieces_kernel(shape, place_ref, counts_ref, *refs):
    group_count, piece_count, _, slot_pad = shape
    block_refs, out_refs = refs[:piece_count], refs[piece_count:]
    rows = block_refs[0].shape[0]
    for piece, block_ref in enumerate(block_refs):
        select = select_matrix(
            lambda group, piece=piece: counts_ref[piece, group],
            place_ref[2],
            group_count,
            slot_pad,
            rows,
        )
        slots = lax.dot_general(
            select, block_ref[...], TN, preferred_element_type=jnp.float32
        ).astype(jnp.bfloat16)
        for step, out_ref in enumerate(out_refs):
            out_ref[piece * slot_pad : (piece + 1) * slot_pad, :] = slots[
                step * slot_pad : (step + 1) * slot_pad, :
            ]


def place_kernel(block_ref, out_ref, sems):
    wait_all(run_copies([(block_ref, out_ref)], sems))


def finish_kernel(shape, whole, place_ref, *refs):
    _, piece_count, _, _ = shape
    sems = refs[-1]
    key_refs, query_refs = refs[:piece_count], refs[piece_count:-3]
    query_out, key_out = refs[-3:-1]
    me, mine = place_ref[0], place_ref[2]
    width = key_refs[0].shape[1]
    if whole:
        pairs = [(query_refs[0], query_out)]
    else:
        pairs = [
            (query_ref, query_out.at[mine ^ step]) for step, query_ref in enumerate(query_refs)
        ]
    pairs += [
        (key_ref, key_out.at[:, aligned(me ^ step, width)]) for step, key_ref in enumerate(key_refs)
    ]
    wait_all(run_copies(pairs, sems))


def gather_blocks(me, block_refs, scratch_ref):
    rows = block_refs[0].shape[0]
    for step, block_ref in enumerate(block_refs):
        scratch_ref[aligned(me ^ step, rows), :] = block_ref[...]


def spread_blocks(me, scratch_ref, out_refs):
    rows = out_refs[0].shape[0]
    for step, out_ref in enumerate(out_refs):
        out_ref[...] = scratch_ref[aligned(me ^ step, rows), :].astype(out_ref.dtype)


def tile_of(query_piece, key_piece):
    return query_piece * (query_piece + 1) // 2 + key_piece


def weight_kernel(pieces, heads, place_ref, inverse_ref, mask_ref, *refs):
    query_refs, key_refs = refs[:pieces], refs[pieces : 2 * pieces]
    weight_ref, factor_ref, query_all, key_all = refs[2 * pieces :]
    me, length = place_ref[0], place_ref[1]
    rows = query_refs[0].shape[0]
    blocks = rows // BLOCK
    size = query_all.shape[1] // heads
    gather_blocks(me, query_refs, query_all)
    gather_blocks(me, key_refs, key_all)
    inverse = inverse_ref[0]
    lanes = lax.broadcasted_iota(jnp.int32, (1, rows), 1)
    for query_piece in range(pieces):
        inside = query_piece * rows + lanes < length
        for key_piece in range(query_piece + 1):
            live = []
            for key_sub in range(blocks):
                level = jnp.zeros((1, rows), jnp.float32)
                for query_sub in range(blocks):
                    query_block = query_piece * blocks + query_sub
                    key_block = key_piece * blocks + key_sub
                    if query_block == key_block:
                        flag = inverse
                    else:
                        flag = jnp.where(mask_ref[query_block, key_block] > 0, inverse, 0.0)
                    level = jnp.where(lanes // BLOCK == query_sub, flag, level)
                level = jnp.where(inside, level, 0.0)
                if query_piece == key_piece:
                    key_ids = key_sub * BLOCK + lax.broadcasted_iota(jnp.int32, (BLOCK, rows), 0)
                    query_ids = lax.broadcasted_iota(jnp.int32, (BLOCK, rows), 1)
                    level = jnp.where(key_ids <= query_ids, level, 0.0)
                live.append(level)
            tile = tile_of(query_piece, key_piece)
            for head in range(heads):
                columns = slice(head * size, (head + 1) * size)
                raw = lax.dot_general(
                    key_all[key_piece * rows : (key_piece + 1) * rows, columns],
                    query_all[query_piece * rows : (query_piece + 1) * rows, columns],
                    NT,
                    preferred_element_type=jnp.float32,
                )
                for key_sub in range(blocks):
                    part = slice(key_sub * BLOCK, (key_sub + 1) * BLOCK)
                    scores = raw[part] * (size ** (-0.5))
                    sigmoid = 1.0 / (1.0 + jnp.exp(-scores))
                    weight_ref[head, tile, part, :] = (scores * sigmoid * live[key_sub]).astype(
                        weight_ref.dtype
                    )
                    factor_ref[head, tile, part, :] = (
                        sigmoid * (1.0 + scores * (1.0 - sigmoid)) * live[key_sub]
                    )


def value_kernel(pieces, heads, place_ref, weight_ref, *refs):
    grad_refs = refs[:pieces]
    out_refs = refs[pieces : 2 * pieces]
    grad_all, value_sum = refs[2 * pieces :]
    me = place_ref[0]
    rows = grad_refs[0].shape[0]
    size = grad_all.shape[1] // heads
    gather_blocks(me, grad_refs, grad_all)
    for head in range(heads):
        columns = slice(head * size, (head + 1) * size)
        for key_piece in range(pieces):
            total = None
            for query_piece in range(key_piece, pieces):
                part = jnp.dot(
                    weight_ref[head, tile_of(query_piece, key_piece)],
                    grad_all[query_piece * rows : (query_piece + 1) * rows, columns],
                    preferred_element_type=jnp.float32,
                )
                total = part if total is None else total + part
            value_sum[key_piece * rows : (key_piece + 1) * rows, columns] = total
    spread_blocks(me, value_sum, out_refs)


def score_kernel(pieces, heads, place_ref, factor_ref, query_all, key_all, grad_all, *refs):
    value_refs = refs[:pieces]
    query_refs, key_refs = refs[pieces : 2 * pieces], refs[2 * pieces : 3 * pieces]
    value_all, query_sum, key_sum, held = refs[3 * pieces :]
    me = place_ref[0]
    rows = value_refs[0].shape[0]
    size = query_all.shape[1] // heads
    scale = size ** (-0.5)
    gather_blocks(me, value_refs, value_all)

    def part(piece):
        return slice(piece * rows, (piece + 1) * rows)

    for head in range(heads):
        columns = slice(head * size, (head + 1) * size)
        for query_piece in range(pieces):
            count = query_piece + 1
            first = tile_of(query_piece, 0)
            products = lax.dot_general(
                value_all[: count * rows, columns],
                grad_all[part(query_piece), columns],
                NT,
                preferred_element_type=jnp.float32,
            )
            factor = factor_ref[head, first : first + count].reshape(count * rows, rows)
            score_grad = (products * factor).astype(jnp.bfloat16)
            held[head, first : first + count] = score_grad.reshape(count, rows, rows)
            total = lax.dot_general(
                score_grad, key_all[: count * rows, columns], TN, preferred_element_type=jnp.float32
            )
            query_sum[part(query_piece), columns] = (total * scale).astype(jnp.bfloat16)
        for key_piece in range(pieces):
            total = None
            for query_piece in range(key_piece, pieces):
                term = jnp.dot(
                    held[head, tile_of(query_piece, key_piece)],
                    query_all[part(query_piece), columns],
                    preferred_element_type=jnp.float32,
                )
                total = term if total is None else total + term
            key_sum[part(key_piece), columns] = (total * scale).astype(jnp.bfloat16)
    spread_blocks(me, query_sum, query_refs)
    spread_blocks(me, key_sum, key_refs)


def local(queries, keys, values, gates, attended, out_grad, plan, hist_len, block_mask):
    group_count = lax.axis_size("dp")
    piece_count = lax.axis_size("seq")
    capacity = queries.shape[2]
    model_width = queries.shape[3]
    slot_count = capacity // group_count
    slot_pad = -(-slot_count // TILE) * TILE
    row_count = ROWS
    head_per = HEADS // piece_count
    width = model_width // piece_count
    full_len = row_count * piece_count
    tile_count = piece_count * (piece_count + 1) // 2
    shape = (group_count, piece_count, slot_count, slot_pad)
    inverse = 1.0 / jnp.sqrt(hist_len.astype(jnp.float32))
    mask = block_mask[0]

    def like(*dims, dtype=jnp.bfloat16):
        return jax.ShapeDtypeStruct(dims, dtype)

    def by_slots(array):
        grouped = array.reshape(group_count, slot_count, model_width)
        if slot_pad > slot_count:
            grouped = jnp.pad(grouped, ((0, 0), (0, slot_pad - slot_count), (0, 0)))
        return grouped

    def exchange(blocks, axis):
        result = [blocks[0]]
        for step in range(1, len(blocks)):
            pairs = [(source, source ^ step) for source in range(len(blocks))]
            result.append(lax.ppermute(blocks[step], axis, pairs))
        return result

    def over_seq(blocks):
        return exchange(blocks, "seq")

    def over_dp(blocks, name):
        if name not in WHOLE:
            return exchange(blocks, "dp")
        (block,) = blocks
        return [
            lax.all_to_all(
                block.reshape(group_count, -1, block.shape[-1]),
                "dp",
                split_axis=0,
                concat_axis=0,
                tiled=True,
            )
        ]

    def to_history(blocks, name):
        blocks = over_dp(blocks, name)
        if name in WHOLE:
            blocks = [blocks[0].reshape(capacity, model_width)]
        return over_seq(
            call(
                functools.partial(unpack_kernel, shape, name not in WHOLE),
                [place] + blocks,
                [like(row_count, width)] * piece_count,
                [pltpu.VMEM((group_count * slot_pad, model_width), jnp.bfloat16)],
                scalars=1,
            ),
        )

    def from_history(blocks, name):
        blocks = over_seq(blocks)
        whole = name in WHOLE
        blocks = call(
            functools.partial(pack_kernel, shape, not whole),
            [place] + blocks,
            [like(capacity, model_width)] if whole else [like(slot_pad, model_width)] * group_count,
            scalars=1,
        )
        return over_dp(blocks, name)

    padded = group_count * slot_pad
    *key_pieces, place = call(
        functools.partial(split_kernel, group_count),
        [hist_len, by_slots(keys).reshape(padded, model_width), plan],
        [like(padded + TILE, width)] * piece_count
        + [like(FIELDS + 2 * group_count, dtype=jnp.int32)],
        [
            pltpu.SMEM(plan.shape, jnp.int32),
            pltpu.VMEM((padded, model_width), jnp.bfloat16),
            pltpu.SemaphoreType.DMA((CUTS,)),
            pltpu.SemaphoreType.DMA((1,)),
        ],
        scalars=1,
        far_in=2,
        scalar_out=1,
    )
    key_pieces = over_seq(key_pieces)

    grouped = (group_count, slot_count, model_width)
    whole = "v" in WHOLE
    gate_grad, attn_grad, *value_slots = call(
        functools.partial(norm_kernel, group_count),
        [place]
        + [array.reshape(grouped) for array in (out_grad, gates, attended)]
        + [by_slots(values)],
        [like(*grouped)] * 2 + [like(slot_pad, model_width)] * (0 if whole else group_count),
        [
            pltpu.VMEM((3,) + grouped, jnp.bfloat16),
            pltpu.VMEM((2,) + grouped, jnp.bfloat16),
            pltpu.SemaphoreType.DMA((PARTS, 3)),
            pltpu.SemaphoreType.DMA((PARTS, 2)),
            pltpu.SemaphoreType.DMA((group_count,)),
        ],
        scalars=1,
        far_in=4,
        far_out=2,
    )

    query_blocks = to_history([queries], "q")
    value_blocks = to_history([values] if whole else value_slots, "v")
    grad_blocks = to_history([attn_grad], "g")

    counts = jnp.concatenate(
        [piece[padded : padded + 1, :group_count] for piece in key_pieces], axis=0
    ).astype(jnp.int32)
    key_groups = over_dp(
        call(
            functools.partial(regroup_kernel, shape),
            [place] + key_pieces,
            [like(piece_count * slot_pad, width)] * group_count,
            scalars=1,
        ),
        "k",
    )
    key_blocks = call(
        functools.partial(unpack_pieces_kernel, shape),
        [place, counts] + key_groups,
        [like(row_count, width)] * piece_count,
        [pltpu.VMEM((piece_count, padded, width), jnp.bfloat16)],
        scalars=2,
    )

    all_bf16 = pltpu.VMEM((full_len, width), jnp.bfloat16)
    all_f32 = pltpu.VMEM((full_len, width), jnp.float32)
    tiles = (head_per, tile_count, row_count, row_count)
    whole_history = like(full_len, width)
    weight, factor, query_all, key_all = call(
        functools.partial(weight_kernel, piece_count, head_per),
        [place, inverse, mask] + query_blocks + key_blocks,
        [like(*tiles), like(*tiles, dtype=jnp.float32), whole_history, whole_history],
        scalars=3,
    )
    *value_grads, grad_all = call(
        functools.partial(value_kernel, piece_count, head_per),
        [place, weight] + grad_blocks,
        [like(row_count, width)] * piece_count + [whole_history],
        [all_f32],
        scalars=1,
    )
    score_grads = call(
        functools.partial(score_kernel, piece_count, head_per),
        [place, factor, query_all, key_all, grad_all] + value_blocks,
        [like(row_count, width)] * (2 * piece_count),
        [all_bf16] * 3 + [pltpu.VMEM(tiles, jnp.bfloat16)],
        scalars=1,
    )

    key_groups = over_dp(
        call(
            functools.partial(pack_pieces_kernel, shape),
            [place, counts] + score_grads[piece_count:],
            [like(piece_count * slot_pad, width)] * group_count,
            scalars=2,
        ),
        "dk",
    )
    value_out = from_history(value_grads, "dv")
    query_out = from_history(score_grads[:piece_count], "dq")
    key_pieces = over_seq(
        call(
            functools.partial(ungroup_kernel, shape),
            [place] + key_groups,
            [like(padded, width)] * piece_count,
            scalars=1,
        ),
    )
    (value_out,) = call(
        place_kernel,
        value_out,
        [like(*value_out[0].shape)],
        [pltpu.SemaphoreType.DMA((1,))],
        far_out=1,
    )
    whole = "dq" in WHOLE
    query_out, key_out = call(
        functools.partial(finish_kernel, shape, whole),
        [place] + key_pieces + query_out,
        [
            like(group_count, slot_count if whole else slot_pad, model_width),
            like(padded, model_width),
        ],
        [pltpu.SemaphoreType.DMA((group_count + piece_count,))],
        scalars=1,
        far_out=2,
    )
    key_out = key_out.reshape(group_count, slot_pad, model_width)
    out_shape = (1, 1, capacity, model_width)
    return (
        query_out[:, :slot_count].reshape(out_shape),
        key_out[:, :slot_count].reshape(out_shape),
        value_out.reshape(out_shape),
        gate_grad.reshape(out_shape),
    )


def solution(mesh):
    rows_spec = P("dp", "seq", None, None)
    in_specs = (rows_spec,) * 6 + (P(None, "seq", None), P("dp"), P("dp", None, None))
    return jax.shard_map(
        local, mesh=mesh, in_specs=in_specs, out_specs=(rows_spec,) * 4, check_vma=False
    )
```
